32 devices in a mesh: tm: 16 (over z, x, core), acct: 2 (over y).
Axes of the slice: x: 2, y: 2, z: 4, core: 2. Of those that a mesh axis runs over, the one named last changes fastest.
Arguments:
- returns: bfloat16 [128, 131072], P('tm'), may hold values from -6 to 6
- start: int32 [1], replicated, may hold values from 0 to 131056
- exposures: bfloat16 [512, 131072], P('acct', 'tm'), may hold values from -0.125 to 0.125
- links: int32 [512], replicated, may hold values from 0 to 127
Outputs:
- cov_block: bfloat16 [16, 131072], P('acct', 'tm')
- house_totals: float32 [16, 128], replicated
The draws below stay inside these ranges and needn't reach their ends.
All inputs are finite; a program needn't handle non-finite values.
Results may differ from the reference program's by a relative error of at most 0.005.
Values may be sent and summed in bfloat16 or wider, within the bound.
A program may use at most 64 MiB of HBM per device.

```python
import math
import jax
import jax.numpy as jnp
from jax import lax

F = 131072
HOUSES = 128
DAYS = 128
B = 16
A = 512


def plant(values, own_key, least, largest):
    dims = values.shape
    spot = [jax.random.randint(jax.random.fold_in(own_key, axis), (), 0, dims[axis]) for axis in range(len(dims))]
    values = values.at[tuple(spot)].set(least)
    longest = dims.index(max(dims))
    spot[longest] = (spot[longest] + 1) % dims[longest]
    return values.at[tuple(spot)].set(largest)


def levels(stream_key, dims, pieces, low, high):
    factor_of = 1.0
    for axis_at, shards_of in pieces:
        draws = jax.random.uniform(jax.random.fold_in(jax.random.fold_in(stream_key, 6), axis_at), (shards_of,), jnp.float32, low / len(pieces), high / len(pieces))
        factor_of = factor_of * jnp.repeat(jnp.exp(draws), dims[axis_at] // shards_of).reshape((-1,) + (1,) * (len(dims) - 1 - axis_at))
    return factor_of


def scatter_about(own_key, extent, deviation, most, shards=(), held_as=jnp.bfloat16):
    factor_of = levels(own_key, extent, shards, -0.22, 0.18) if shards else 1.0
    entries = jax.random.normal(own_key, extent, jnp.float32) * deviation * factor_of
    return jnp.minimum(jnp.maximum(entries, -most), most).astype(held_as)


def setup_inputs(seed: int = 0) -> dict:
    key_list = jax.random.split(jax.random.key(seed), 5)
    return {
        "returns": scatter_about(key_list[0], (DAYS, F), 1.0, 6.0, ((0, 16),)),
        "start": jax.random.randint(key_list[1], (1,), 0, F - B + 1).astype(jnp.int32),
        "exposures": scatter_about(key_list[2], (A, F), (F // 64) ** -0.5, 0.125, ((0, 2), (1, 16))),
        "links": plant(jax.random.randint(key_list[3], (A,), 0, HOUSES), jax.random.fold_in(key_list[3], 1), 0, HOUSES - 1).astype(jnp.int32),
    }


def day_weights(total_days):
    days = jnp.arange(total_days, dtype=jnp.float32)
    raw = jnp.exp(-math.log(3.0) * (total_days - 1.0 - days) / total_days)
    return raw / jnp.sum(raw)


def reference(returns, start, exposures, links):
    weights = day_weights(returns.shape[0])
    rows = lax.dynamic_slice_in_dim(returns, start[0].astype(jnp.int32), B, 1)
    block = (rows.astype(jnp.float32) * weights[:, None]).astype(jnp.bfloat16)
    cov_block = lax.dot_general(block, returns, (((0,), (0,)), ((), ())), preferred_element_type=jnp.float32).astype(jnp.bfloat16)
    loads = lax.dot_general(cov_block, exposures, (((1,), (1,)), ((), ())), preferred_element_type=jnp.float32)
    onehot = (links[:, None] == jnp.arange(HOUSES, dtype=jnp.int32)[None, :]).astype(jnp.float32)
    house_totals = jnp.dot(loads, onehot, precision=lax.Precision.HIGHEST)
    return cov_block, house_totals
```

```python
import functools
import math

import jax
import jax.numpy as jnp
from jax import lax
from jax.experimental import pallas as pl
from jax.experimental.pallas import tpu as pltpu
from jax.sharding import PartitionSpec as P

HOUSES = 128
LANES = 128
MESH = pl.DeviceIdType.MESH


def near_root(count):
    return max(d for d in range(1, count + 1) if count % d == 0 and d * d <= count)


def kernel(
    sizes,
    picked_ref, links_ref, returns_hbm, exposures_hbm,
    cov_ref, totals_ref,
    exps, gathered, blocks, turned, slots1, slots2,
    local_sem, dsend, drecv, bsend, brecv, fsend, frecv, send1, recv1, send2, recv2,
):
    tms, accts, low, rows_dev = sizes
    days, factors = returns_hbm.shape
    all_days = days * tms
    rows = rows_dev * accts
    cols = factors // tms
    piece = cols // accts
    own_accounts = exps.shape[0]
    me, acct = lax.axis_index("tm"), lax.axis_index("acct")
    place, layer = lax.rem(me, low), me // low

    def there(shift):
        return lax.rem(me + shift, tms)

    def at_acct(shift):
        return lax.rem(acct + shift, accts)

    own_cols = pl.ds(pl.multiple_of(me * cols, LANES), cols)
    load_own = pltpu.make_async_copy(returns_hbm.at[:, own_cols], gathered.at[me], local_sem.at[0])
    load_own.start()
    load_exps = pltpu.make_async_copy(exposures_hbm, exps, local_sem.at[1])
    load_exps.start()

    barrier = pltpu.get_barrier_semaphore()
    greeted = 0
    for shift in range(1, tms):
        pl.semaphore_signal(barrier, inc=1, device_id=(there(shift), acct), device_id_type=MESH)
        greeted += 1
    for step in range(low):
        for hop in range(1, accts):
            other = layer * low + lax.rem(place + step, low)
            pl.semaphore_signal(barrier, inc=1, device_id=(other, at_acct(hop)), device_id_type=MESH)
            greeted += 1

    def raw_weight(day):
        return jnp.exp(-math.log(3.0) * (all_days - 1.0 - day.astype(jnp.float32)) / all_days)

    total = jnp.sum(
        raw_weight(lax.broadcasted_iota(jnp.int32, (days, all_days), 1)), axis=1, keepdims=True
    )
    weights = raw_weight(me * days + lax.broadcasted_iota(jnp.int32, (days, LANES), 0)) / total
    blocks[me] = (picked_ref[...].astype(jnp.float32) * weights).astype(jnp.bfloat16)

    pl.semaphore_wait(barrier, greeted)

    shifts = sorted(range(1, tms), key=lambda s: -min(s, tms - s))
    own_piece = pl.ds(pl.multiple_of(acct * piece, LANES), piece)
    sends = []
    for shift in shifts:
        copy = pltpu.make_async_remote_copy(
            src_ref=blocks.at[me], dst_ref=blocks.at[me],
            send_sem=bsend.at[shift], recv_sem=brecv.at[shift],
            device_id=(there(shift), acct), device_id_type=MESH,
        )
        copy.start()
        sends.append(copy)
    for shift in shifts:
        to = there(shift)
        out_cols = pl.ds(pl.multiple_of(to * cols + acct * piece, LANES), piece)
        copy = pltpu.make_async_remote_copy(
            src_ref=returns_hbm.at[:, out_cols], dst_ref=gathered.at[me, :, own_piece],
            send_sem=dsend.at[shift], recv_sem=drecv.at[shift],
            device_id=(to, acct), device_id_type=MESH,
        )
        copy.start()
        sends.append(copy)

    def slab(shift, part):
        return gathered.at[there(tms - shift), :, pl.ds(pl.multiple_of(part * piece, LANES), piece)]

    for shift in shifts:
        held = slab(shift, acct)
        pltpu.make_async_remote_copy(
            src_ref=held, dst_ref=held, send_sem=dsend.at[shift], recv_sem=drecv.at[shift],
            device_id=(there(shift), acct), device_id_type=MESH,
        ).wait_recv()
        for hop in range(1, accts):
            copy = pltpu.make_async_remote_copy(
                src_ref=held, dst_ref=held,
                send_sem=fsend.at[hop, shift], recv_sem=frecv.at[hop, shift],
                device_id=(me, at_acct(hop)), device_id_type=MESH,
            )
            copy.start()
            sends.append(copy)

    for shift in shifts:
        block = blocks.at[there(tms - shift)]
        pltpu.make_async_remote_copy(
            src_ref=block, dst_ref=block, send_sem=bsend.at[shift], recv_sem=brecv.at[shift],
            device_id=(there(shift), acct), device_id_type=MESH,
        ).wait_recv()
    turned[...] = blocks[...].astype(jnp.float32).reshape(all_days, LANES).T
    own_rows = turned[pl.ds(pl.multiple_of(acct * rows_dev, rows_dev), rows_dev), :]
    left = jnp.concatenate([turned[:rows, :], own_rows], axis=0).astype(jnp.bfloat16)
    load_own.wait()
    load_exps.wait()

    width = min(piece, 1024)
    loads = jnp.zeros((rows, own_accounts), jnp.float32)
    for turn in range(accts):
        part = at_acct(turn)
        if turn:
            hop = accts - turn
            for shift in shifts:
                held = slab(shift, part)
                pltpu.make_async_remote_copy(
                    src_ref=held, dst_ref=held,
                    send_sem=fsend.at[hop, shift], recv_sem=frecv.at[hop, shift],
                    device_id=(me, at_acct(hop)), device_id_type=MESH,
                ).wait_recv()
        for at in range(0, piece, width):
            span = pl.ds(pl.multiple_of(part * piece + at, LANES), width)
            tile = gathered[:, :, span].astype(jnp.float32).reshape(all_days, width)
            cov = jnp.dot(
                left, tile.astype(jnp.bfloat16), preferred_element_type=jnp.float32
            )
            cov_ref[:, span] = cov[rows:].astype(jnp.bfloat16)
            loads += lax.dot_general(
                cov[:rows].astype(jnp.bfloat16), exps[:, span], (((1,), (1,)), ((), ())),
                preferred_element_type=jnp.float32,
            )

    links = links_ref[:, pl.ds(pl.multiple_of(acct * own_accounts, LANES), own_accounts)]
    house = lax.broadcasted_iota(jnp.int32, (HOUSES, own_accounts), 0)
    member = jnp.where(house == links, 1.0, 0.0)
    mine = place * accts + acct
    slots1[mine] = lax.dot_general(
        loads, member, (((1,), (1,)), ((), ())),
        precision=lax.Precision.HIGHEST, preferred_element_type=jnp.float32,
    )

    group = low * accts
    for step in range(1, group):
        other = layer * low + lax.rem(place + step // accts, low)
        copy = pltpu.make_async_remote_copy(
            src_ref=slots1.at[mine], dst_ref=slots1.at[mine],
            send_sem=send1.at[step], recv_sem=recv1.at[step],
            device_id=(other, at_acct(step % accts)), device_id_type=MESH,
        )
        copy.start()
        sends.append(copy)
    for step in range(1, group):
        sender = lax.rem(place + low - step // accts, low) * accts + at_acct(accts - step % accts)
        pltpu.make_async_remote_copy(
            src_ref=slots1.at[sender], dst_ref=slots1.at[sender],
            send_sem=send1.at[step], recv_sem=recv1.at[step],
            device_id=(me, at_acct(accts - 1)), device_id_type=MESH,
        ).wait_recv()
    slots2[layer] = jnp.sum(slots1[...], axis=0)
    layers = tms // low
    for step in range(1, layers):
        copy = pltpu.make_async_remote_copy(
            src_ref=slots2.at[layer], dst_ref=slots2.at[layer],
            send_sem=send2.at[step], recv_sem=recv2.at[step],
            device_id=(lax.rem(layer + step, layers) * low + place, acct), device_id_type=MESH,
        )
        copy.start()
        sends.append(copy)
    for step in range(1, layers):
        sender = lax.rem(layer + layers - step, layers)
        pltpu.make_async_remote_copy(
            src_ref=slots2.at[sender], dst_ref=slots2.at[sender],
            send_sem=send2.at[step], recv_sem=recv2.at[step],
            device_id=(me, at_acct(accts - 1)), device_id_type=MESH,
        ).wait_recv()
    totals_ref[...] = jnp.sum(slots2[...], axis=0)
    for copy in sends:
        copy.wait_send()


def on_device(tms, accts, returns, start, exposures, links):
    days, factors = returns.shape
    own_accounts, cols = exposures.shape
    rows_dev = 8
    rows = rows_dev * accts
    low = near_root(tms)
    picked = lax.dynamic_slice_in_dim(returns, start[0], rows, 1)
    picked = jnp.pad(picked, ((0, 0), (0, LANES - rows)))
    dma = pltpu.SemaphoreType.DMA
    return pl.pallas_call(
        functools.partial(kernel, (tms, accts, low, rows_dev)),
        out_shape=(
            jax.ShapeDtypeStruct((rows_dev, cols), jnp.bfloat16),
            jax.ShapeDtypeStruct((rows, HOUSES), jnp.float32),
        ),
        in_specs=[
            pl.BlockSpec(memory_space=pltpu.VMEM),
            pl.BlockSpec(memory_space=pltpu.VMEM),
            pl.BlockSpec(memory_space=pl.ANY),
            pl.BlockSpec(memory_space=pl.ANY),
        ],
        out_specs=(
            pl.BlockSpec(memory_space=pltpu.VMEM),
            pl.BlockSpec(memory_space=pltpu.VMEM),
        ),
        scratch_shapes=[
            pltpu.VMEM((own_accounts, cols), exposures.dtype),
            pltpu.VMEM((tms, days, cols), returns.dtype),
            pltpu.VMEM((tms, days, LANES), jnp.bfloat16),
            pltpu.VMEM((LANES, days * tms), jnp.float32),
            pltpu.VMEM((low * accts, rows, HOUSES), jnp.float32),
            pltpu.VMEM((tms // low, rows, HOUSES), jnp.float32),
            dma((2,)),
            dma((tms,)), dma((tms,)), dma((tms,)), dma((tms,)),
            dma((accts, tms)), dma((accts, tms)),
            dma((low * accts,)), dma((low * accts,)),
            dma((tms // low,)), dma((tms // low,)),
        ],
        compiler_params=pltpu.CompilerParams(collective_id=0, has_side_effects=True),
        name="exposures_by_house",
    )(picked, links[None, :], returns, exposures)


def solution(mesh):
    return jax.shard_map(
        functools.partial(on_device, mesh.shape["tm"], mesh.shape["acct"]),
        mesh=mesh,
        in_specs=(P("tm", None), P(), P("acct", "tm"), P()),
        out_specs=(P("acct", "tm"), P()),
        check_vma=False,
    )
```

```python
import functools
import math

import jax
import jax.numpy as jnp
from jax import lax
from jax.experimental import pallas as pl
from jax.experimental.pallas import tpu as pltpu
from jax.sharding import PartitionSpec as P

HOUSES = 128
LANES = 128
MESH = pl.DeviceIdType.MESH


def near_root(count):
    return max(d for d in range(1, count + 1) if count % d == 0 and d * d <= count)


def kernel(
    sizes,
    start_ref, window_ref, links_ref, returns_hbm, exposures_hbm,
    cov_hbm, totals_ref,
    exps, gathered, blocks, turned, covs, slots1, slots2,
    local_sem, dsend, drecv, bsend, brecv, fsend, frecv, send1, recv1, send2, recv2,
):
    tms, accts, low, rows_dev = sizes
    days, factors = returns_hbm.shape
    all_days = days * tms
    rows = rows_dev * accts
    cols = factors // tms
    piece = cols // accts
    own_accounts = exps.shape[0]
    me, acct = lax.axis_index("tm"), lax.axis_index("acct")
    place, layer = lax.rem(me, low), me // low

    def there(shift):
        return lax.rem(me + shift, tms)

    def at_acct(shift):
        return lax.rem(acct + shift, accts)

    own_cols = pl.ds(pl.multiple_of(me * cols + acct * piece, LANES), piece)
    load_own = pltpu.make_async_copy(returns_hbm.at[:, own_cols], gathered.at[me], local_sem.at[0])
    load_own.start()
    load_exps = pltpu.make_async_copy(exposures_hbm, exps, local_sem.at[1])
    load_exps.start()

    barrier = pltpu.get_barrier_semaphore()
    greeted = 0
    for shift in range(1, tms):
        pl.semaphore_signal(barrier, inc=1, device_id=(there(shift), acct), device_id_type=MESH)
        greeted += 1
    for step in range(low):
        for hop in range(1, accts):
            other = layer * low + lax.rem(place + step, low)
            pl.semaphore_signal(barrier, inc=1, device_id=(other, at_acct(hop)), device_id_type=MESH)
            greeted += 1

    offset = start_ref[0] - jnp.minimum(start_ref[0], factors - LANES)
    source = lax.broadcasted_iota(jnp.int32, (LANES, LANES), 0)
    target = lax.broadcasted_iota(jnp.int32, (LANES, LANES), 1)
    pick = jnp.where((source == target + offset) & (target < rows), 1.0, 0.0)
    picked = jnp.dot(
        window_ref[...], pick.astype(jnp.bfloat16), preferred_element_type=jnp.float32
    )
    def raw_weight(day):
        return jnp.exp(-math.log(3.0) * (all_days - 1.0 - day.astype(jnp.float32)) / all_days)

    total = jnp.sum(
        raw_weight(lax.broadcasted_iota(jnp.int32, (days, all_days), 1)), axis=1, keepdims=True
    )
    weights = raw_weight(me * days + lax.broadcasted_iota(jnp.int32, (days, LANES), 0)) / total
    blocks[me] = (picked * weights).astype(jnp.bfloat16)

    pl.semaphore_wait(barrier, greeted)

    shifts = sorted(range(1, tms), key=lambda s: -min(s, tms - s))
    sends = []
    for shift in shifts:
        copy = pltpu.make_async_remote_copy(
            src_ref=blocks.at[me], dst_ref=blocks.at[me],
            send_sem=bsend.at[shift], recv_sem=brecv.at[shift],
            device_id=(there(shift), acct), device_id_type=MESH,
        )
        copy.start()
        sends.append(copy)
    last = max(LANES, piece // 4 // LANES * LANES)
    parts = [(at, size) for at, size in ((0, piece - last), (piece - last, last)) if size]

    def direct(index, shift, slot):
        at, size = parts[index]
        to = there(shift)
        return pltpu.make_async_remote_copy(
            src_ref=returns_hbm.at[
                :, pl.ds(pl.multiple_of(to * cols + acct * piece + at, LANES), size)
            ],
            dst_ref=gathered.at[slot, :, pl.ds(at, size)],
            send_sem=dsend.at[index, shift], recv_sem=drecv.at[index, shift],
            device_id=(to, acct), device_id_type=MESH,
        )

    for index in range(len(parts)):
        for shift in shifts:
            copy = direct(index, shift, me)
            copy.start()
            sends.append(copy)

    for shift in shifts:
        block = blocks.at[there(tms - shift)]
        pltpu.make_async_remote_copy(
            src_ref=block, dst_ref=block, send_sem=bsend.at[shift], recv_sem=brecv.at[shift],
            device_id=(there(shift), acct), device_id_type=MESH,
        ).wait_recv()
    turned[...] = blocks[...].astype(jnp.float32).reshape(all_days, LANES).T
    left = turned[:rows, :].astype(jnp.bfloat16)
    load_own.wait()
    load_exps.wait()

    def columns(owner, at, size):
        return pl.ds(pl.multiple_of(owner * piece + at, LANES), size)

    def exchange(index, hop, owner):
        held = covs.at[:, :, columns(owner, *parts[index])]
        return pltpu.make_async_remote_copy(
            src_ref=held, dst_ref=held,
            send_sem=fsend.at[index, hop], recv_sem=frecv.at[index, hop],
            device_id=(me, at_acct(hop)), device_id_type=MESH,
        )

    def loads_of(owner, index):
        span = columns(owner, *parts[index])
        cov = covs[:, :, span].astype(jnp.float32).reshape(rows, parts[index][1])
        return lax.dot_general(
            cov.astype(jnp.bfloat16), exps[:, span], (((1,), (1,)), ((), ())),
            preferred_element_type=jnp.float32,
        )

    loads = jnp.zeros((rows, own_accounts), jnp.float32)
    for index, (first, size) in enumerate(parts):
        for shift in shifts:
            direct(index, shift, there(tms - shift)).wait_recv()
        width = math.gcd(size, 1024)
        for at in range(first, first + size, width):
            tile = gathered[:, :, pl.ds(at, width)].astype(jnp.float32)
            cov = jnp.dot(
                left, tile.reshape(all_days, width).astype(jnp.bfloat16),
                preferred_element_type=jnp.float32,
            )
            covs[:, :, columns(acct, at, width)] = cov.reshape(accts, rows_dev, width).astype(
                jnp.bfloat16
            )
        for hop in range(1, accts):
            copy = exchange(index, hop, acct)
            copy.start()
            sends.append(copy)
        loads += loads_of(acct, index)
        for hop in range(1, accts):
            owner = at_acct(accts - hop)
            exchange(index, hop, owner).wait_recv()
            loads += loads_of(owner, index)
    store_cov = pltpu.make_async_copy(covs.at[acct], cov_hbm, local_sem.at[0])
    store_cov.start()

    links = links_ref[:, pl.ds(pl.multiple_of(acct * own_accounts, LANES), own_accounts)]
    house = lax.broadcasted_iota(jnp.int32, (HOUSES, own_accounts), 0)
    member = jnp.where(house == links, 1.0, 0.0)
    mine = place * accts + acct
    slots1[mine] = lax.dot_general(
        loads, member, (((1,), (1,)), ((), ())),
        precision=lax.Precision.HIGHEST, preferred_element_type=jnp.float32,
    )

    group = low * accts
    for step in range(1, group):
        other = layer * low + lax.rem(place + step // accts, low)
        copy = pltpu.make_async_remote_copy(
            src_ref=slots1.at[mine], dst_ref=slots1.at[mine],
            send_sem=send1.at[step], recv_sem=recv1.at[step],
            device_id=(other, at_acct(step % accts)), device_id_type=MESH,
        )
        copy.start()
        sends.append(copy)
    for step in range(1, group):
        sender = lax.rem(place + low - step // accts, low) * accts + at_acct(accts - step % accts)
        pltpu.make_async_remote_copy(
            src_ref=slots1.at[sender], dst_ref=slots1.at[sender],
            send_sem=send1.at[step], recv_sem=recv1.at[step],
            device_id=(me, at_acct(accts - 1)), device_id_type=MESH,
        ).wait_recv()
    slots2[layer] = jnp.sum(slots1[...], axis=0)
    layers = tms // low
    for step in range(1, layers):
        copy = pltpu.make_async_remote_copy(
            src_ref=slots2.at[layer], dst_ref=slots2.at[layer],
            send_sem=send2.at[step], recv_sem=recv2.at[step],
            device_id=(lax.rem(layer + step, layers) * low + place, acct), device_id_type=MESH,
        )
        copy.start()
        sends.append(copy)
    for step in range(1, layers):
        sender = lax.rem(layer + layers - step, layers)
        pltpu.make_async_remote_copy(
            src_ref=slots2.at[sender], dst_ref=slots2.at[sender],
            send_sem=send2.at[step], recv_sem=recv2.at[step],
            device_id=(me, at_acct(accts - 1)), device_id_type=MESH,
        ).wait_recv()
    totals_ref[...] = jnp.sum(slots2[...], axis=0)
    for copy in sends:
        copy.wait_send()
    store_cov.wait()


def on_device(tms, accts, returns, start, exposures, links):
    days, factors = returns.shape
    own_accounts, cols = exposures.shape
    rows_dev = 8
    rows = rows_dev * accts
    low = near_root(tms)
    window = lax.dynamic_slice_in_dim(
        returns, jnp.minimum(start[0], factors - LANES), LANES, 1
    )
    dma = pltpu.SemaphoreType.DMA
    return pl.pallas_call(
        functools.partial(kernel, (tms, accts, low, rows_dev)),
        out_shape=(
            jax.ShapeDtypeStruct((rows_dev, cols), jnp.bfloat16),
            jax.ShapeDtypeStruct((rows, HOUSES), jnp.float32),
        ),
        in_specs=[
            pl.BlockSpec(memory_space=pltpu.SMEM),
            pl.BlockSpec(memory_space=pltpu.VMEM),
            pl.BlockSpec(memory_space=pltpu.VMEM),
            pl.BlockSpec(memory_space=pl.ANY),
            pl.BlockSpec(memory_space=pl.ANY),
        ],
        out_specs=(
            pl.BlockSpec(memory_space=pl.ANY),
            pl.BlockSpec(memory_space=pltpu.VMEM),
        ),
        scratch_shapes=[
            pltpu.VMEM((own_accounts, cols), exposures.dtype),
            pltpu.VMEM((tms, days, cols // accts), returns.dtype),
            pltpu.VMEM((tms, days, LANES), jnp.bfloat16),
            pltpu.VMEM((LANES, days * tms), jnp.float32),
            pltpu.VMEM((accts, rows_dev, cols), jnp.bfloat16),
            pltpu.VMEM((low * accts, rows, HOUSES), jnp.float32),
            pltpu.VMEM((tms // low, rows, HOUSES), jnp.float32),
            dma((2,)),
            dma((2, tms)), dma((2, tms)), dma((tms,)), dma((tms,)),
            dma((2, accts)), dma((2, accts)),
            dma((low * accts,)), dma((low * accts,)),
            dma((tms // low,)), dma((tms // low,)),
        ],
        compiler_params=pltpu.CompilerParams(collective_id=0, has_side_effects=True),
        name="exposures_by_house",
    )(start, window, links[None, :], returns, exposures)


def solution(mesh):
    return jax.shard_map(
        functools.partial(on_device, mesh.shape["tm"], mesh.shape["acct"]),
        mesh=mesh,
        in_specs=(P("tm", None), P(), P("acct", "tm"), P()),
        out_specs=(P("acct", "tm"), P()),
        check_vma=False,
    )
```

```python
import functools
import math

import jax
import jax.numpy as jnp
from jax import lax
from jax.experimental import pallas as pl
from jax.experimental.pallas import tpu as pltpu
from jax.sharding import PartitionSpec as P

HOUSES = 128
LANES = 128
MESH = pl.DeviceIdType.MESH


def near_root(count):
    return max(d for d in range(1, count + 1) if count % d == 0 and d * d <= count)


def kernel(
    sizes,
    start_ref, links_ref, tiles_hbm, returns_hbm, exposures_hbm,
    cov_hbm, totals_ref,
    tiles, exps, gathered, blocks, turned, covs, slots1, slots2,
    local_sem, dsend, drecv, bsend, brecv, fsend, frecv, send1, recv1, send2, recv2,
):
    tms, accts, low, rows_dev = sizes
    days, factors = returns_hbm.shape
    all_days = days * tms
    rows = rows_dev * accts
    cols = factors // tms
    piece = cols // accts
    own_accounts = exps.shape[0]
    me, acct = lax.axis_index("tm"), lax.axis_index("acct")
    place, layer = lax.rem(me, low), me // low

    def there(shift):
        return lax.rem(me + shift, tms)

    def at_acct(shift):
        return lax.rem(acct + shift, accts)

    own_cols = pl.ds(pl.multiple_of(me * cols + acct * piece, LANES), piece)
    load_tiles = pltpu.make_async_copy(tiles_hbm, tiles, local_sem.at[2])
    load_tiles.start()
    load_own = pltpu.make_async_copy(returns_hbm.at[:, own_cols], gathered.at[me], local_sem.at[0])
    load_own.start()
    load_exps = pltpu.make_async_copy(exposures_hbm, exps, local_sem.at[1])
    load_exps.start()

    barrier = pltpu.get_barrier_semaphore()
    greeted = 0
    for shift in range(1, tms):
        pl.semaphore_signal(barrier, inc=1, device_id=(there(shift), acct), device_id_type=MESH)
        greeted += 1
    for step in range(low):
        for hop in range(1, accts):
            other = layer * low + lax.rem(place + step, low)
            pl.semaphore_signal(barrier, inc=1, device_id=(other, at_acct(hop)), device_id_type=MESH)
            greeted += 1

    load_tiles.wait()
    tile_count = tiles.shape[0]
    first_tile = lax.div(start_ref[0], LANES)
    window = jnp.concatenate(
        [tiles[first_tile], tiles[jnp.minimum(first_tile + 1, tile_count - 1)]], axis=1
    )
    offset = start_ref[0] - first_tile * LANES
    source = lax.broadcasted_iota(jnp.int32, (2 * LANES, LANES), 0)
    target = lax.broadcasted_iota(jnp.int32, (2 * LANES, LANES), 1)
    pick = jnp.where((source == target + offset) & (target < rows), 1.0, 0.0)
    picked = jnp.dot(window, pick.astype(jnp.bfloat16), preferred_element_type=jnp.float32)

    def raw_weight(day):
        return jnp.exp(-math.log(3.0) * (all_days - 1.0 - day.astype(jnp.float32)) / all_days)

    total = jnp.sum(
        raw_weight(lax.broadcasted_iota(jnp.int32, (days, all_days), 1)), axis=1, keepdims=True
    )
    weights = raw_weight(me * days + lax.broadcasted_iota(jnp.int32, (days, LANES), 0)) / total
    blocks[me] = (picked * weights).astype(jnp.bfloat16)

    pl.semaphore_wait(barrier, greeted)

    shifts = sorted(range(1, tms), key=lambda s: -min(s, tms - s))
    sends = []
    for shift in shifts:
        copy = pltpu.make_async_remote_copy(
            src_ref=blocks.at[me], dst_ref=blocks.at[me],
            send_sem=bsend.at[shift], recv_sem=brecv.at[shift],
            device_id=(there(shift), acct), device_id_type=MESH,
        )
        copy.start()
        sends.append(copy)
    last = max(LANES, piece // 4 // LANES * LANES)
    parts = [(at, size) for at, size in ((0, piece - last), (piece - last, last)) if size]

    def direct(index, shift, slot):
        at, size = parts[index]
        to = there(shift)
        return pltpu.make_async_remote_copy(
            src_ref=returns_hbm.at[
                :, pl.ds(pl.multiple_of(to * cols + acct * piece + at, LANES), size)
            ],
            dst_ref=gathered.at[slot, :, pl.ds(at, size)],
            send_sem=dsend.at[index, shift], recv_sem=drecv.at[index, shift],
            device_id=(to, acct), device_id_type=MESH,
        )

    for index in range(len(parts)):
        for shift in shifts:
            copy = direct(index, shift, me)
            copy.start()
            sends.append(copy)

    for shift in shifts:
        block = blocks.at[there(tms - shift)]
        pltpu.make_async_remote_copy(
            src_ref=block, dst_ref=block, send_sem=bsend.at[shift], recv_sem=brecv.at[shift],
            device_id=(there(shift), acct), device_id_type=MESH,
        ).wait_recv()
    turned[...] = blocks[...].astype(jnp.float32).reshape(all_days, LANES).T
    left = turned[:rows, :].astype(jnp.bfloat16)
    load_own.wait()
    load_exps.wait()

    def columns(owner, at, size):
        return pl.ds(pl.multiple_of(owner * piece + at, LANES), size)

    def exchange(index, hop, owner):
        held = covs.at[:, :, columns(owner, *parts[index])]
        return pltpu.make_async_remote_copy(
            src_ref=held, dst_ref=held,
            send_sem=fsend.at[index, hop], recv_sem=frecv.at[index, hop],
            device_id=(me, at_acct(hop)), device_id_type=MESH,
        )

    def loads_of(owner, index):
        span = columns(owner, *parts[index])
        cov = covs[:, :, span].astype(jnp.float32).reshape(rows, parts[index][1])
        return lax.dot_general(
            cov.astype(jnp.bfloat16), exps[:, span], (((1,), (1,)), ((), ())),
            preferred_element_type=jnp.float32,
        )

    loads = jnp.zeros((rows, own_accounts), jnp.float32)
    for index, (first, size) in enumerate(parts):
        for shift in shifts:
            direct(index, shift, there(tms - shift)).wait_recv()
        width = math.gcd(size, 1024)
        for at in range(first, first + size, width):
            tile = gathered[:, :, pl.ds(at, width)].astype(jnp.float32)
            cov = jnp.dot(
                left, tile.reshape(all_days, width).astype(jnp.bfloat16),
                preferred_element_type=jnp.float32,
            )
            covs[:, :, columns(acct, at, width)] = cov.reshape(accts, rows_dev, width).astype(
                jnp.bfloat16
            )
        for hop in range(1, accts):
            copy = exchange(index, hop, acct)
            copy.start()
            sends.append(copy)
        loads += loads_of(acct, index)
        for hop in range(1, accts):
            owner = at_acct(accts - hop)
            exchange(index, hop, owner).wait_recv()
            loads += loads_of(owner, index)
    store_cov = pltpu.make_async_copy(covs.at[acct], cov_hbm, local_sem.at[0])
    store_cov.start()

    links = links_ref[:, pl.ds(pl.multiple_of(acct * own_accounts, LANES), own_accounts)]
    house = lax.broadcasted_iota(jnp.int32, (HOUSES, own_accounts), 0)
    member = jnp.where(house == links, 1.0, 0.0)
    mine = place * accts + acct
    slots1[mine] = lax.dot_general(
        loads, member, (((1,), (1,)), ((), ())),
        precision=lax.Precision.HIGHEST, preferred_element_type=jnp.float32,
    )

    group = low * accts
    for step in range(1, group):
        other = layer * low + lax.rem(place + step // accts, low)
        copy = pltpu.make_async_remote_copy(
            src_ref=slots1.at[mine], dst_ref=slots1.at[mine],
            send_sem=send1.at[step], recv_sem=recv1.at[step],
            device_id=(other, at_acct(step % accts)), device_id_type=MESH,
        )
        copy.start()
        sends.append(copy)
    for step in range(1, group):
        sender = lax.rem(place + low - step // accts, low) * accts + at_acct(accts - step % accts)
        pltpu.make_async_remote_copy(
            src_ref=slots1.at[sender], dst_ref=slots1.at[sender],
            send_sem=send1.at[step], recv_sem=recv1.at[step],
            device_id=(me, at_acct(accts - 1)), device_id_type=MESH,
        ).wait_recv()
    slots2[layer] = jnp.sum(slots1[...], axis=0)
    layers = tms // low
    for step in range(1, layers):
        copy = pltpu.make_async_remote_copy(
            src_ref=slots2.at[layer], dst_ref=slots2.at[layer],
            send_sem=send2.at[step], recv_sem=recv2.at[step],
            device_id=(lax.rem(layer + step, layers) * low + place, acct), device_id_type=MESH,
        )
        copy.start()
        sends.append(copy)
    for step in range(1, layers):
        sender = lax.rem(layer + layers - step, layers)
        pltpu.make_async_remote_copy(
            src_ref=slots2.at[sender], dst_ref=slots2.at[sender],
            send_sem=send2.at[step], recv_sem=recv2.at[step],
            device_id=(me, at_acct(accts - 1)), device_id_type=MESH,
        ).wait_recv()
    totals_ref[...] = jnp.sum(slots2[...], axis=0)
    for copy in sends:
        copy.wait_send()
    store_cov.wait()


def hand_over(cov_ref, totals_ref, cov_out, totals_out):
    cov_out[...] = cov_ref[...]
    totals_out[...] = totals_ref[...]


def on_device(tms, accts, returns, start, exposures, links):
    days, factors = returns.shape
    own_accounts, cols = exposures.shape
    rows_dev = 8
    rows = rows_dev * accts
    low = near_root(tms)
    tiles = returns.reshape(days, factors // LANES, LANES).transpose(1, 0, 2)
    dma = pltpu.SemaphoreType.DMA
    cov, totals = pl.pallas_call(
        functools.partial(kernel, (tms, accts, low, rows_dev)),
        out_shape=(
            jax.ShapeDtypeStruct((rows_dev, cols), jnp.bfloat16),
            jax.ShapeDtypeStruct((rows, HOUSES), jnp.float32),
        ),
        in_specs=[
            pl.BlockSpec(memory_space=pltpu.SMEM),
            pl.BlockSpec(memory_space=pltpu.VMEM),
            pl.BlockSpec(memory_space=pl.ANY),
            pl.BlockSpec(memory_space=pl.ANY),
            pl.BlockSpec(memory_space=pl.ANY),
        ],
        out_specs=(
            pl.BlockSpec(memory_space=pl.ANY),
            pl.BlockSpec(memory_space=pltpu.VMEM),
        ),
        scratch_shapes=[
            pltpu.VMEM((factors // LANES, days, LANES), returns.dtype),
            pltpu.VMEM((own_accounts, cols), exposures.dtype),
            pltpu.VMEM((tms, days, cols // accts), returns.dtype),
            pltpu.VMEM((tms, days, LANES), jnp.bfloat16),
            pltpu.VMEM((LANES, days * tms), jnp.float32),
            pltpu.VMEM((accts, rows_dev, cols), jnp.bfloat16),
            pltpu.VMEM((low * accts, rows, HOUSES), jnp.float32),
            pltpu.VMEM((tms // low, rows, HOUSES), jnp.float32),
            dma((3,)),
            dma((2, tms)), dma((2, tms)), dma((tms,)), dma((tms,)),
            dma((2, accts)), dma((2, accts)),
            dma((low * accts,)), dma((low * accts,)),
            dma((tms // low,)), dma((tms // low,)),
        ],
        compiler_params=pltpu.CompilerParams(collective_id=0, has_side_effects=True),
        name="exposures_by_house",
    )(start, links[None, :], tiles, returns, exposures)
    return pl.pallas_call(
        hand_over,
        out_shape=(
            jax.ShapeDtypeStruct(cov.shape, cov.dtype),
            jax.ShapeDtypeStruct(totals.shape, totals.dtype),
        ),
        in_specs=[pl.BlockSpec(memory_space=pltpu.VMEM)] * 2,
        out_specs=(pl.BlockSpec(memory_space=pltpu.VMEM),) * 2,
        name="hand_over",
    )(cov, totals)


def solution(mesh):
    return jax.shard_map(
        functools.partial(on_device, mesh.shape["tm"], mesh.shape["acct"]),
        mesh=mesh,
        in_specs=(P("tm", None), P(), P("acct", "tm"), P()),
        out_specs=(P("acct", "tm"), P()),
        check_vma=False,
    )
```

```python
import functools
import math

import jax
import jax.numpy as jnp
from jax import lax
from jax.experimental import pallas as pl
from jax.experimental.pallas import tpu as pltpu
from jax.sharding import PartitionSpec as P

HOUSES = 128
LANES = 128
MESH = pl.DeviceIdType.MESH


def near_root(count):
    return max(d for d in range(1, count + 1) if count % d == 0 and d * d <= count)


def kernel(
    sizes,
    start_ref, links_ref, tiles_hbm, returns_hbm, exposures_hbm,
    cov_hbm, totals_ref,
    tiles, exps, gathered, blocks, turned, covs, slots1, slots2,
    local_sem, dsend, drecv, bsend, brecv, fsend, frecv, send1, recv1, send2, recv2,
):
    tms, accts, low, rows_dev = sizes
    days, factors = returns_hbm.shape
    all_days = days * tms
    rows = rows_dev * accts
    cols = factors // tms
    piece = cols // accts
    own_accounts = exps.shape[0]
    me, acct = lax.axis_index("tm"), lax.axis_index("acct")
    place, layer = lax.rem(me, low), me // low

    def there(shift):
        return lax.rem(me + shift, tms)

    def at_acct(shift):
        return lax.rem(acct + shift, accts)

    own_cols = pl.ds(pl.multiple_of(me * cols + acct * piece, LANES), piece)
    load_tiles = pltpu.make_async_copy(tiles_hbm, tiles, local_sem.at[2])
    load_tiles.start()
    load_own = pltpu.make_async_copy(returns_hbm.at[:, own_cols], gathered.at[me], local_sem.at[0])
    load_own.start()
    load_exps = pltpu.make_async_copy(exposures_hbm, exps, local_sem.at[1])
    load_exps.start()

    barrier = pltpu.get_barrier_semaphore()
    greeted = 0
    for shift in range(1, tms):
        pl.semaphore_signal(barrier, inc=1, device_id=(there(shift), acct), device_id_type=MESH)
        greeted += 1
    for step in range(low):
        for hop in range(1, accts):
            other = layer * low + lax.rem(place + step, low)
            pl.semaphore_signal(barrier, inc=1, device_id=(other, at_acct(hop)), device_id_type=MESH)
            greeted += 1

    load_tiles.wait()
    tile_count = tiles.shape[0]
    first_tile = lax.div(start_ref[0], LANES)
    window = jnp.concatenate(
        [tiles[first_tile], tiles[jnp.minimum(first_tile + 1, tile_count - 1)]], axis=1
    )
    offset = start_ref[0] - first_tile * LANES
    source = lax.broadcasted_iota(jnp.int32, (2 * LANES, LANES), 0)
    target = lax.broadcasted_iota(jnp.int32, (2 * LANES, LANES), 1)
    pick = jnp.where((source == target + offset) & (target < rows), 1.0, 0.0)
    picked = jnp.dot(window, pick.astype(jnp.bfloat16), preferred_element_type=jnp.float32)

    def raw_weight(day):
        return jnp.exp(-math.log(3.0) * (all_days - 1.0 - day.astype(jnp.float32)) / all_days)

    total = jnp.sum(
        raw_weight(lax.broadcasted_iota(jnp.int32, (days, all_days), 1)), axis=1, keepdims=True
    )
    weights = raw_weight(me * days + lax.broadcasted_iota(jnp.int32, (days, LANES), 0)) / total
    blocks[me] = (picked * weights).astype(jnp.bfloat16)

    pl.semaphore_wait(barrier, greeted)

    shifts = [*range(tms // 2, tms), *range(tms // 2 - 1, 0, -1)]
    sends = []
    for shift in shifts:
        copy = pltpu.make_async_remote_copy(
            src_ref=blocks.at[me], dst_ref=blocks.at[me],
            send_sem=bsend.at[shift], recv_sem=brecv.at[shift],
            device_id=(there(shift), acct), device_id_type=MESH,
        )
        copy.start()
        sends.append(copy)
    last = max(LANES, piece // 2 // LANES * LANES)
    parts = [(at, size) for at, size in ((0, piece - last), (piece - last, last)) if size]

    def direct(index, shift, slot):
        at, size = parts[index]
        to = there(shift)
        return pltpu.make_async_remote_copy(
            src_ref=returns_hbm.at[
                :, pl.ds(pl.multiple_of(to * cols + acct * piece + at, LANES), size)
            ],
            dst_ref=gathered.at[slot, :, pl.ds(at, size)],
            send_sem=dsend.at[index, shift], recv_sem=drecv.at[index, shift],
            device_id=(to, acct), device_id_type=MESH,
        )

    for index in range(len(parts)):
        for shift in shifts:
            copy = direct(index, shift, me)
            copy.start()
            sends.append(copy)

    for shift in shifts:
        block = blocks.at[there(tms - shift)]
        pltpu.make_async_remote_copy(
            src_ref=block, dst_ref=block, send_sem=bsend.at[shift], recv_sem=brecv.at[shift],
            device_id=(there(shift), acct), device_id_type=MESH,
        ).wait_recv()
    turned[...] = blocks[...].astype(jnp.float32).reshape(all_days, LANES).T
    left = turned[:rows, :].astype(jnp.bfloat16)
    load_own.wait()
    load_exps.wait()

    def columns(owner, at, size):
        return pl.ds(pl.multiple_of(owner * piece + at, LANES), size)

    def exchange(index, hop, owner):
        held = covs.at[:, :, columns(owner, *parts[index])]
        return pltpu.make_async_remote_copy(
            src_ref=held, dst_ref=held,
            send_sem=fsend.at[index, hop], recv_sem=frecv.at[index, hop],
            device_id=(me, at_acct(hop)), device_id_type=MESH,
        )

    def loads_of(owner, index):
        span = columns(owner, *parts[index])
        cov = covs[:, :, span].astype(jnp.float32).reshape(rows, parts[index][1])
        return lax.dot_general(
            cov.astype(jnp.bfloat16), exps[:, span], (((1,), (1,)), ((), ())),
            preferred_element_type=jnp.float32,
        )

    loads = jnp.zeros((rows, own_accounts), jnp.float32)
    for index, (first, size) in enumerate(parts):
        for shift in shifts:
            direct(index, shift, there(tms - shift)).wait_recv()
        width = math.gcd(size, 1024)
        for at in range(first, first + size, width):
            tile = gathered[:, :, pl.ds(at, width)].astype(jnp.float32)
            cov = jnp.dot(
                left, tile.reshape(all_days, width).astype(jnp.bfloat16),
                preferred_element_type=jnp.float32,
            )
            covs[:, :, columns(acct, at, width)] = cov.reshape(accts, rows_dev, width).astype(
                jnp.bfloat16
            )
        for hop in range(1, accts):
            copy = exchange(index, hop, acct)
            copy.start()
            sends.append(copy)
        loads += loads_of(acct, index)
        for hop in range(1, accts):
            owner = at_acct(accts - hop)
            exchange(index, hop, owner).wait_recv()
            loads += loads_of(owner, index)
    store_cov = pltpu.make_async_copy(covs.at[acct], cov_hbm, local_sem.at[0])
    store_cov.start()

    links = links_ref[:, pl.ds(pl.multiple_of(acct * own_accounts, LANES), own_accounts)]
    house = lax.broadcasted_iota(jnp.int32, (HOUSES, own_accounts), 0)
    member = jnp.where(house == links, 1.0, 0.0)
    mine = place * accts + acct
    slots1[mine] = lax.dot_general(
        loads, member, (((1,), (1,)), ((), ())),
        precision=lax.Precision.HIGHEST, preferred_element_type=jnp.float32,
    )

    group = low * accts
    for step in range(1, group):
        other = layer * low + lax.rem(place + step // accts, low)
        copy = pltpu.make_async_remote_copy(
            src_ref=slots1.at[mine], dst_ref=slots1.at[mine],
            send_sem=send1.at[step], recv_sem=recv1.at[step],
            device_id=(other, at_acct(step % accts)), device_id_type=MESH,
        )
        copy.start()
        sends.append(copy)
    for step in range(1, group):
        sender = lax.rem(place + low - step // accts, low) * accts + at_acct(accts - step % accts)
        pltpu.make_async_remote_copy(
            src_ref=slots1.at[sender], dst_ref=slots1.at[sender],
            send_sem=send1.at[step], recv_sem=recv1.at[step],
            device_id=(me, at_acct(accts - 1)), device_id_type=MESH,
        ).wait_recv()
    slots2[layer] = jnp.sum(slots1[...], axis=0)
    layers = tms // low
    for step in range(1, layers):
        copy = pltpu.make_async_remote_copy(
            src_ref=slots2.at[layer], dst_ref=slots2.at[layer],
            send_sem=send2.at[step], recv_sem=recv2.at[step],
            device_id=(lax.rem(layer + step, layers) * low + place, acct), device_id_type=MESH,
        )
        copy.start()
        sends.append(copy)
    for step in range(1, layers):
        sender = lax.rem(layer + layers - step, layers)
        pltpu.make_async_remote_copy(
            src_ref=slots2.at[sender], dst_ref=slots2.at[sender],
            send_sem=send2.at[step], recv_sem=recv2.at[step],
            device_id=(me, at_acct(accts - 1)), device_id_type=MESH,
        ).wait_recv()
    totals_ref[...] = jnp.sum(slots2[...], axis=0)
    for copy in sends:
        copy.wait_send()
    store_cov.wait()


def hand_over(cov_ref, totals_ref, cov_out, totals_out):
    cov_out[...] = cov_ref[...]
    totals_out[...] = totals_ref[...]


def on_device(tms, accts, returns, start, exposures, links):
    days, factors = returns.shape
    own_accounts, cols = exposures.shape
    rows_dev = 8
    rows = rows_dev * accts
    low = near_root(tms)
    tiles = returns.reshape(days, factors // LANES, LANES).transpose(1, 0, 2)
    dma = pltpu.SemaphoreType.DMA
    cov, totals = pl.pallas_call(
        functools.partial(kernel, (tms, accts, low, rows_dev)),
        out_shape=(
            jax.ShapeDtypeStruct((rows_dev, cols), jnp.bfloat16),
            jax.ShapeDtypeStruct((rows, HOUSES), jnp.float32),
        ),
        in_specs=[
            pl.BlockSpec(memory_space=pltpu.SMEM),
            pl.BlockSpec(memory_space=pltpu.VMEM),
            pl.BlockSpec(memory_space=pl.ANY),
            pl.BlockSpec(memory_space=pl.ANY),
            pl.BlockSpec(memory_space=pl.ANY),
        ],
        out_specs=(
            pl.BlockSpec(memory_space=pl.ANY),
            pl.BlockSpec(memory_space=pltpu.VMEM),
        ),
        scratch_shapes=[
            pltpu.VMEM((factors // LANES, days, LANES), returns.dtype),
            pltpu.VMEM((own_accounts, cols), exposures.dtype),
            pltpu.VMEM((tms, days, cols // accts), returns.dtype),
            pltpu.VMEM((tms, days, LANES), jnp.bfloat16),
            pltpu.VMEM((LANES, days * tms), jnp.float32),
            pltpu.VMEM((accts, rows_dev, cols), jnp.bfloat16),
            pltpu.VMEM((low * accts, rows, HOUSES), jnp.float32),
            pltpu.VMEM((tms // low, rows, HOUSES), jnp.float32),
            dma((3,)),
            dma((2, tms)), dma((2, tms)), dma((tms,)), dma((tms,)),
            dma((2, accts)), dma((2, accts)),
            dma((low * accts,)), dma((low * accts,)),
            dma((tms // low,)), dma((tms // low,)),
        ],
        compiler_params=pltpu.CompilerParams(collective_id=0, has_side_effects=True),
        name="exposures_by_house",
    )(start, links[None, :], tiles, returns, exposures)
    return pl.pallas_call(
        hand_over,
        out_shape=(
            jax.ShapeDtypeStruct(cov.shape, cov.dtype),
            jax.ShapeDtypeStruct(totals.shape, totals.dtype),
        ),
        in_specs=[pl.BlockSpec(memory_space=pltpu.VMEM)] * 2,
        out_specs=(pl.BlockSpec(memory_space=pltpu.VMEM),) * 2,
        name="hand_over",
    )(cov, totals)


def solution(mesh):
    return jax.shard_map(
        functools.partial(on_device, mesh.shape["tm"], mesh.shape["acct"]),
        mesh=mesh,
        in_specs=(P("tm", None), P(), P("acct", "tm"), P()),
        out_specs=(P("acct", "tm"), P()),
        check_vma=False,
    )
```

```python
import functools
import math

import jax
import jax.numpy as jnp
from jax import lax
from jax.experimental import pallas as pl
from jax.experimental.pallas import tpu as pltpu
from jax.sharding import PartitionSpec as P

HOUSES = 128
LANES = 128
MESH = pl.DeviceIdType.MESH


def least_divisor(count):
    return min((d for d in range(2, count + 1) if count % d == 0), default=1)


def kernel(
    sizes,
    start_ref, links_ref, tiles_hbm, returns_hbm, exposures_hbm,
    cov_hbm, totals_ref,
    tiles, exps, gathered, blocks, turned, covs, slots1, slots2,
    local_sem, dsend, drecv, bsend, brecv, fsend, frecv, send1, recv1, send2, recv2,
):
    tms, accts, low, rows_dev = sizes
    days, factors = returns_hbm.shape
    all_days = days * tms
    rows = rows_dev * accts
    cols = factors // tms
    piece = cols // accts
    own_accounts = exps.shape[0]
    me, acct = lax.axis_index("tm"), lax.axis_index("acct")
    place, layer = lax.rem(me, low), me // low

    def there(shift):
        return lax.rem(me + shift, tms)

    def at_acct(shift):
        return lax.rem(acct + shift, accts)

    own_cols = pl.ds(pl.multiple_of(me * cols + acct * piece, LANES), piece)
    load_tiles = pltpu.make_async_copy(tiles_hbm, tiles, local_sem.at[2])
    load_tiles.start()
    load_own = pltpu.make_async_copy(returns_hbm.at[:, own_cols], gathered.at[me], local_sem.at[0])
    load_own.start()
    load_exps = pltpu.make_async_copy(exposures_hbm, exps, local_sem.at[1])
    load_exps.start()

    barrier = pltpu.get_barrier_semaphore()
    greeted = 0
    for shift in range(1, tms):
        pl.semaphore_signal(barrier, inc=1, device_id=(there(shift), acct), device_id_type=MESH)
        greeted += 1
    for step in range(low):
        for hop in range(1, accts):
            other = layer * low + lax.rem(place + step, low)
            pl.semaphore_signal(barrier, inc=1, device_id=(other, at_acct(hop)), device_id_type=MESH)
            greeted += 1

    load_tiles.wait()
    tile_count = tiles.shape[0]
    first_tile = lax.div(start_ref[0], LANES)
    window = jnp.concatenate(
        [tiles[first_tile], tiles[jnp.minimum(first_tile + 1, tile_count - 1)]], axis=1
    )
    offset = start_ref[0] - first_tile * LANES
    source = lax.broadcasted_iota(jnp.int32, (2 * LANES, LANES), 0)
    target = lax.broadcasted_iota(jnp.int32, (2 * LANES, LANES), 1)
    pick = jnp.where((source == target + offset) & (target < rows), 1.0, 0.0)
    picked = jnp.dot(window, pick.astype(jnp.bfloat16), preferred_element_type=jnp.float32)

    def raw_weight(day):
        return jnp.exp(-math.log(3.0) * (all_days - 1.0 - day.astype(jnp.float32)) / all_days)

    total = jnp.sum(
        raw_weight(lax.broadcasted_iota(jnp.int32, (days, all_days), 1)), axis=1, keepdims=True
    )
    weights = raw_weight(me * days + lax.broadcasted_iota(jnp.int32, (days, LANES), 0)) / total
    blocks[me] = (picked * weights).astype(jnp.bfloat16)

    pl.semaphore_wait(barrier, greeted)

    shifts = [*range(tms // 2, tms), *range(tms // 2 - 1, 0, -1)]
    sends = []
    for shift in shifts:
        copy = pltpu.make_async_remote_copy(
            src_ref=blocks.at[me], dst_ref=blocks.at[me],
            send_sem=bsend.at[shift], recv_sem=brecv.at[shift],
            device_id=(there(shift), acct), device_id_type=MESH,
        )
        copy.start()
        sends.append(copy)
    last = max(LANES, piece // 2 // LANES * LANES)
    parts = [(at, size) for at, size in ((0, piece - last), (piece - last, last)) if size]

    def direct(index, shift, slot):
        at, size = parts[index]
        to = there(shift)
        return pltpu.make_async_remote_copy(
            src_ref=returns_hbm.at[
                :, pl.ds(pl.multiple_of(to * cols + acct * piece + at, LANES), size)
            ],
            dst_ref=gathered.at[slot, :, pl.ds(at, size)],
            send_sem=dsend.at[index, shift], recv_sem=drecv.at[index, shift],
            device_id=(to, acct), device_id_type=MESH,
        )

    for index in range(len(parts)):
        for shift in shifts:
            copy = direct(index, shift, me)
            copy.start()
            sends.append(copy)

    for shift in shifts:
        block = blocks.at[there(tms - shift)]
        pltpu.make_async_remote_copy(
            src_ref=block, dst_ref=block, send_sem=bsend.at[shift], recv_sem=brecv.at[shift],
            device_id=(there(shift), acct), device_id_type=MESH,
        ).wait_recv()
    turned[...] = blocks[...].astype(jnp.float32).reshape(all_days, LANES).T
    left = turned[:rows, :].astype(jnp.bfloat16)
    load_own.wait()
    load_exps.wait()

    def columns(owner, at, size):
        return pl.ds(pl.multiple_of(owner * piece + at, LANES), size)

    def exchange(index, hop, owner):
        held = covs.at[:, :, columns(owner, *parts[index])]
        return pltpu.make_async_remote_copy(
            src_ref=held, dst_ref=held,
            send_sem=fsend.at[index, hop], recv_sem=frecv.at[index, hop],
            device_id=(me, at_acct(hop)), device_id_type=MESH,
        )

    def loads_of(owner, index):
        span = columns(owner, *parts[index])
        cov = covs[:, :, span].astype(jnp.float32).reshape(rows, parts[index][1])
        return lax.dot_general(
            cov.astype(jnp.bfloat16), exps[:, span], (((1,), (1,)), ((), ())),
            preferred_element_type=jnp.float32,
        )

    loads = jnp.zeros((rows, own_accounts), jnp.float32)
    for index, (first, size) in enumerate(parts):
        for shift in shifts:
            direct(index, shift, there(tms - shift)).wait_recv()
        width = math.gcd(size, 1024)
        for at in range(first, first + size, width):
            tile = gathered[:, :, pl.ds(at, width)].astype(jnp.float32)
            cov = jnp.dot(
                left, tile.reshape(all_days, width).astype(jnp.bfloat16),
                preferred_element_type=jnp.float32,
            )
            covs[:, :, columns(acct, at, width)] = cov.reshape(accts, rows_dev, width).astype(
                jnp.bfloat16
            )
        for hop in range(1, accts):
            copy = exchange(index, hop, acct)
            copy.start()
            sends.append(copy)
        loads += loads_of(acct, index)
        for hop in range(1, accts):
            owner = at_acct(accts - hop)
            exchange(index, hop, owner).wait_recv()
            loads += loads_of(owner, index)
    store_cov = pltpu.make_async_copy(covs.at[acct], cov_hbm, local_sem.at[0])
    store_cov.start()

    links = links_ref[:, pl.ds(pl.multiple_of(acct * own_accounts, LANES), own_accounts)]
    house = lax.broadcasted_iota(jnp.int32, (HOUSES, own_accounts), 0)
    member = jnp.where(house == links, 1.0, 0.0)
    mine = place * accts + acct
    slots1[mine] = lax.dot_general(
        loads, member, (((1,), (1,)), ((), ())),
        precision=lax.Precision.HIGHEST, preferred_element_type=jnp.float32,
    )

    group = low * accts
    for step in range(1, group):
        other = layer * low + lax.rem(place + step // accts, low)
        copy = pltpu.make_async_remote_copy(
            src_ref=slots1.at[mine], dst_ref=slots1.at[mine],
            send_sem=send1.at[step], recv_sem=recv1.at[step],
            device_id=(other, at_acct(step % accts)), device_id_type=MESH,
        )
        copy.start()
        sends.append(copy)
    for step in range(1, group):
        sender = lax.rem(place + low - step // accts, low) * accts + at_acct(accts - step % accts)
        pltpu.make_async_remote_copy(
            src_ref=slots1.at[sender], dst_ref=slots1.at[sender],
            send_sem=send1.at[step], recv_sem=recv1.at[step],
            device_id=(me, at_acct(accts - 1)), device_id_type=MESH,
        ).wait_recv()
    slots2[layer] = jnp.sum(slots1[...], axis=0)
    layers = tms // low
    for step in range(1, layers):
        copy = pltpu.make_async_remote_copy(
            src_ref=slots2.at[layer], dst_ref=slots2.at[layer],
            send_sem=send2.at[step], recv_sem=recv2.at[step],
            device_id=(lax.rem(layer + step, layers) * low + place, acct), device_id_type=MESH,
        )
        copy.start()
        sends.append(copy)
    for step in range(1, layers):
        sender = lax.rem(layer + layers - step, layers)
        pltpu.make_async_remote_copy(
            src_ref=slots2.at[sender], dst_ref=slots2.at[sender],
            send_sem=send2.at[step], recv_sem=recv2.at[step],
            device_id=(me, at_acct(accts - 1)), device_id_type=MESH,
        ).wait_recv()
    totals_ref[...] = jnp.sum(slots2[...], axis=0)
    for copy in sends:
        copy.wait_send()
    store_cov.wait()


def hand_over(cov_ref, totals_ref, cov_out, totals_out):
    cov_out[...] = cov_ref[...]
    totals_out[...] = totals_ref[...]


def on_device(tms, accts, returns, start, exposures, links):
    days, factors = returns.shape
    own_accounts, cols = exposures.shape
    rows_dev = 8
    rows = rows_dev * accts
    low = least_divisor(tms)
    tiles = returns.reshape(days, factors // LANES, LANES).transpose(1, 0, 2)
    dma = pltpu.SemaphoreType.DMA
    cov, totals = pl.pallas_call(
        functools.partial(kernel, (tms, accts, low, rows_dev)),
        out_shape=(
            jax.ShapeDtypeStruct((rows_dev, cols), jnp.bfloat16),
            jax.ShapeDtypeStruct((rows, HOUSES), jnp.float32),
        ),
        in_specs=[
            pl.BlockSpec(memory_space=pltpu.SMEM),
            pl.BlockSpec(memory_space=pltpu.VMEM),
            pl.BlockSpec(memory_space=pl.ANY),
            pl.BlockSpec(memory_space=pl.ANY),
            pl.BlockSpec(memory_space=pl.ANY),
        ],
        out_specs=(
            pl.BlockSpec(memory_space=pl.ANY),
            pl.BlockSpec(memory_space=pltpu.VMEM),
        ),
        scratch_shapes=[
            pltpu.VMEM((factors // LANES, days, LANES), returns.dtype),
            pltpu.VMEM((own_accounts, cols), exposures.dtype),
            pltpu.VMEM((tms, days, cols // accts), returns.dtype),
            pltpu.VMEM((tms, days, LANES), jnp.bfloat16),
            pltpu.VMEM((LANES, days * tms), jnp.float32),
            pltpu.VMEM((accts, rows_dev, cols), jnp.bfloat16),
            pltpu.VMEM((low * accts, rows, HOUSES), jnp.float32),
            pltpu.VMEM((tms // low, rows, HOUSES), jnp.float32),
            dma((3,)),
            dma((2, tms)), dma((2, tms)), dma((tms,)), dma((tms,)),
            dma((2, accts)), dma((2, accts)),
            dma((low * accts,)), dma((low * accts,)),
            dma((tms // low,)), dma((tms // low,)),
        ],
        compiler_params=pltpu.CompilerParams(collective_id=0, has_side_effects=True),
        name="exposures_by_house",
    )(start, links[None, :], tiles, returns, exposures)
    return pl.pallas_call(
        hand_over,
        out_shape=(
            jax.ShapeDtypeStruct(cov.shape, cov.dtype),
            jax.ShapeDtypeStruct(totals.shape, totals.dtype),
        ),
        in_specs=[pl.BlockSpec(memory_space=pltpu.VMEM)] * 2,
        out_specs=(pl.BlockSpec(memory_space=pltpu.VMEM),) * 2,
        name="hand_over",
    )(cov, totals)


def solution(mesh):
    return jax.shard_map(
        functools.partial(on_device, mesh.shape["tm"], mesh.shape["acct"]),
        mesh=mesh,
        in_specs=(P("tm", None), P(), P("acct", "tm"), P()),
        out_specs=(P("acct", "tm"), P()),
        check_vma=False,
    )
```
